512 devices in a mesh: group: 8 (over z_lo), shard: 64 (over z_hi, x, y, core).
Axes of the slice: x: 4, y: 4, z: 16 (z_hi: 2, z_lo: 8; z = z_hi * 8 + z_lo), core: 2. Of those that a mesh axis runs over, the one named last changes fastest.
Arguments:
- inner_embed: float32 [8, 15360, 768], P('group', 'shard'), may hold values from -6 to 6
- outer_embed: float32 [15360, 768], P('shard'), may hold values from -6 to 6
- moment_embed: float32 [15360, 768], P('shard'), may hold values from -6 to 6
- basis: float32 [15360, 64], P('shard'), may hold values from -6 to 6
- inner_attn: float32 [8, 768, 3072], P('group', 'shard'), may hold values from -6 to 6
- outer_attn: float32 [768, 3072], P(None, 'shard'), may hold values from -6 to 6
- moment_attn: float32 [768, 3072], P(None, 'shard'), may hold values from -6 to 6
- inner_norms: float32 [8, 4, 768], P('group', None, 'shard'), may hold values from -6 to 6
- outer_norms: float32 [4, 768], P(None, 'shard'), may hold values from -6 to 6
- moment_norms: float32 [4, 768], P(None, 'shard'), may hold values from -6 to 6
Outputs:
- new_embed: float32 [15360, 768], P('shard')
- new_moment_embed: float32 [15360, 768], P('shard')
- new_attn: float32 [768, 3072], P(None, 'shard')
- new_moment_attn: float32 [768, 3072], P(None, 'shard')
- new_norms: float32 [4, 768], P(None, 'shard')
- new_moment_norms: float32 [4, 768], P(None, 'shard')
- replica_attn: bfloat16 [768, 3072], P('shard')
The draws below stay inside these ranges and needn't reach their ends.
All inputs are finite; a program needn't handle non-finite values.
Results may differ from the reference program's by a relative error of at most 0.0004.
Values may be sent and summed in bfloat16 or wider, within the bound.
A program may use at most 64 MiB of HBM per device.

```python
import math
import jax
import jax.numpy as jnp
from jax import lax

D = 768
VOCAB = 15360
RANK = 64
NORMS = 4
GROUPS = 8


def block_scale(own_key, dims, pieces, low, largest):
    factor_of, own = 1.0, jax.random.fold_in(own_key, 6)
    for axis_at, blocks in pieces:
        heights = jnp.exp(jax.random.uniform(jax.random.fold_in(own, axis_at), (blocks,), jnp.float32, low / len(pieces), largest / len(pieces)))
        factor_of = factor_of * jnp.repeat(heights, dims[axis_at] // blocks).reshape([-1 if axis == axis_at else 1 for axis in range(len(dims))])
    return factor_of


def gaussian(own_key, shape, scale, most, split=(), kind=jnp.bfloat16):
    result = jax.random.normal(own_key, shape, jnp.float32) * scale
    if len(split) > 0:
        result = block_scale(own_key, shape, split, -0.22, 0.18) * result
    return jnp.clip(result, min=-most, max=most).astype(kind)


def setup_inputs(seed: int = 0) -> dict:
    streams_of = jax.random.split(jax.random.key(seed), 11)
    inner_embed = gaussian(streams_of[0], (GROUPS, VOCAB, D), 1.0, 6.0, ((0, 8), (1, 64)), jnp.float32)
    outer_embed = gaussian(streams_of[1], (VOCAB, D), 1.0, 6.0, ((0, 64),), jnp.float32)
    moment_embed = gaussian(streams_of[2], (VOCAB, D), 1.0, 6.0, ((0, 64),), jnp.float32)
    basis = gaussian(streams_of[3], (VOCAB, RANK), 1.0, 6.0, ((0, 64),), jnp.float32)
    inner_attn = gaussian(streams_of[4], (GROUPS, D, 4 * D), 1.0, 6.0, ((0, 8), (1, 64)), jnp.float32)
    outer_attn = gaussian(streams_of[5], (D, 4 * D), 1.0, 6.0, ((1, 64),), jnp.float32)
    moment_attn = gaussian(streams_of[6], (D, 4 * D), 1.0, 6.0, ((1, 64),), jnp.float32)
    inner_norms = gaussian(streams_of[7], (GROUPS, NORMS, D), 1.0, 6.0, ((0, 8), (2, 64)), jnp.float32)
    outer_norms = gaussian(streams_of[8], (NORMS, D), 1.0, 6.0, ((1, 64),), jnp.float32)
    moment_norms = gaussian(streams_of[9], (NORMS, D), 1.0, 6.0, ((1, 64),), jnp.float32)
    return dict(inner_embed=inner_embed, outer_embed=outer_embed, moment_embed=moment_embed, basis=basis, inner_attn=inner_attn, outer_attn=outer_attn, moment_attn=moment_attn, inner_norms=inner_norms, outer_norms=outer_norms, moment_norms=moment_norms)


def nesterov(outer, moment, delta):
    moment_new = 0.5 * moment + delta
    return (outer - (delta + 0.5 * moment_new), moment_new)

def reference(inner_embed, outer_embed, moment_embed, basis, inner_attn, outer_attn, moment_attn, inner_norms, outer_norms, moment_norms):
    coefficient = jnp.zeros((RANK, D), jnp.float32)
    for index in range(GROUPS):
        differ = outer_embed - inner_embed[index]
        coefficient = coefficient + jnp.dot(basis.T, differ, precision=lax.Precision.HIGHEST, preferred_element_type=jnp.float32)
    coefficient = coefficient / GROUPS
    embed_delta = jnp.dot(basis, coefficient, precision=lax.Precision.HIGHEST, preferred_element_type=jnp.float32) * (1.0 / math.sqrt(RANK * VOCAB))
    attn_delta = lax.optimization_barrier(jnp.mean(outer_attn[None] - inner_attn, axis=0))
    norm_delta = lax.optimization_barrier(jnp.mean(outer_norms[None] - inner_norms, axis=0))
    new_embed, new_moment_embed = nesterov(outer_embed, moment_embed, embed_delta)
    new_attn, new_moment_attn = nesterov(outer_attn, moment_attn, attn_delta)
    new_norms, new_moment_norms = nesterov(outer_norms, moment_norms, norm_delta)
    replica_attn = new_attn.astype(jnp.bfloat16)
    return (new_embed, new_moment_embed, new_attn, new_moment_attn, new_norms, new_moment_norms, replica_attn)
```

```python
import math

import jax
import jax.numpy as jnp
from jax import lax
from jax.experimental import pallas as pl
from jax.experimental.pallas import tpu as pltpu
from jax.sharding import PartitionSpec as P

VOCAB = 15360
RANK = 64
D = 768
N = 8
ROWS = 12
COLS = 48
WIDE = N * COLS
TALL = N * ROWS
MESH = pl.DeviceIdType.MESH
HIGHEST = lax.Precision.HIGHEST
SCALE = 1.0 / math.sqrt(RANK * VOCAB)

CA, CB, CG, RB, RA, P1, W, NR, SW, AG, RP = range(11)
(L_IE, L_OE, L_BA, L_ME, L_OA, L_MA, L_IA, L_IN, L_ON, L_MN,
 L_EM, L_AT, L_NO, L_RP) = range(14)


def nesterov(outer, moment, delta):
    moment_new = 0.5 * moment + delta
    return (outer - (delta + 0.5 * moment_new), moment_new)


def kernel(
    inner_e, outer_e, mom_e, basis, inner_a, outer_a, mom_a, inner_n, outer_n, mom_n,
    new_e, new_me, new_a, new_ma, new_n, new_mn, rep,
    v_ie, v_oe, v_me, v_ba, v_oa, v_ma, v_on, v_mn,
    r_norm, c_part, r_ca, c_row, r_cb, c_one, r_cg, c_fin, r_rb, c_blk, r_ra,
    r_p1, w_out, r_w, d_out, r_d, d_pack, r_ag, rp_out, r_rp,
    o_e, o_me, o_a, o_ma, o_n, o_mn, o_rep,
    send, recv, once, local,
):
    g = lax.axis_index("group")
    s = lax.axis_index("shard")
    b = s // N
    a = s % N
    over_g = [(lax.rem(g + k, N), s) for k in range(1, N)]
    over_a = [(g, N * b + lax.rem(a + k, N)) for k in range(1, N)]
    over_b = [(g, N * lax.rem(b + k, N) + a) for k in range(1, N)]
    swapped = [(b, N * g + lax.rem(a + k, N)) for k in range(N)]
    crossing = g != b

    def load(src, dst, sem):
        copy = pltpu.make_async_copy(src, dst, local.at[sem])
        copy.start()
        return copy

    ld_oa = load(outer_a, v_oa, L_OA)
    ld_ma = load(mom_a, v_ma, L_MA)
    ld_ie = load(inner_e.at[0], v_ie, L_IE)
    ld_oe = load(outer_e, v_oe, L_OE)
    ld_ba = load(basis, v_ba, L_BA)
    ld_ia = load(
        inner_a.at[0, :, pl.ds(pl.multiple_of(g * WIDE, 128), WIDE)], r_p1.at[g], L_IA
    )
    ld_in = load(inner_n.at[0], r_norm.at[g], L_IN)
    ld_on = load(outer_n, v_on, L_ON)
    ld_mn = load(mom_n, v_mn, L_MN)
    ld_me = load(mom_e, v_me, L_ME)

    barrier = pltpu.get_barrier_semaphore()

    def greet(device):
        pl.semaphore_signal(barrier, inc=1, device_id=device, device_id_type=MESH)

    for device in over_a + over_g + over_b + swapped[1:]:
        greet(device)

    @pl.when(crossing)
    def _():
        greet(swapped[0])

    def put(src, dst, phase, device, send_sem=None):
        pltpu.make_async_remote_copy(
            src_ref=src,
            dst_ref=dst,
            send_sem=send.at[phase] if send_sem is None else send_sem,
            recv_sem=recv.at[phase],
            device_id=device,
            device_id_type=MESH,
        ).start()

    def whole(ref, phase, count):
        part = ref.at[pl.ds(0, count)]
        return pltpu.make_async_remote_copy(
            src_ref=part,
            dst_ref=part,
            send_sem=send.at[phase],
            recv_sem=recv.at[phase],
            device_id=over_g[0],
            device_id_type=MESH,
        )

    def arrived(ref, phase):
        whole(ref, phase, N - 1).wait_recv()

    def swap(src, dst, phase, turn):
        @pl.when(crossing)
        def _():
            put(src.at[a], dst.at[a], phase, swapped[0], once.at[turn])

        @pl.when(jnp.logical_not(crossing))
        def _():
            dst[a] = src[a]

        for k in range(1, N):
            put(src.at[lax.rem(a + k, N)], dst.at[a], phase, swapped[k])

    def swap_arrived(ref, phase):
        @pl.when(crossing)
        def _():
            whole(ref, phase, N).wait_recv()

        @pl.when(jnp.logical_not(crossing))
        def _():
            arrived(ref, phase)

    ld_oa.wait()
    ld_ma.wait()
    mine = pl.ds(pl.multiple_of(g * TALL, 8), TALL)
    outer_block = v_oa[mine, :]
    mom_block = v_ma[mine, :]
    for j in range(N):
        w_out[j, 0] = outer_block[j * ROWS : (j + 1) * ROWS, :]
        w_out[j, 1] = mom_block[j * ROWS : (j + 1) * ROWS, :]

    ld_ie.wait()
    ld_oe.wait()
    ld_ba.wait()
    v_ie[...] = v_oe[...] - v_ie[...]
    part = lax.dot_general(
        v_ba[...],
        v_ie[...],
        (((0,), (0,)), ((), ())),
        precision=HIGHEST,
        preferred_element_type=jnp.float32,
    )
    c_part[...] = part.reshape(N, N, D)

    pl.semaphore_wait(barrier, 4 * (N - 1) + jnp.where(crossing, 1, 0))

    for k in range(1, N):
        put(c_part.at[lax.rem(a + k, N)], r_ca.at[a], CA, over_a[k - 1])
    for k in range(1, N):
        to = lax.rem(g + k, N)
        put(
            inner_a.at[0, :, pl.ds(pl.multiple_of(to * WIDE, 128), WIDE)],
            r_p1.at[g],
            P1,
            over_g[k - 1],
        )
    swap(w_out, r_w, W, 0)
    for k in range(1, N):
        put(inner_n.at[0], r_norm.at[g], NR, over_g[k - 1])

    r_ca[a] = c_part[a]
    arrived(r_ca, CA)
    rows = r_ca[0]
    for j in range(1, N):
        rows = rows + r_ca[j]
    for j in range(N):
        c_row[j] = rows[j : j + 1, :]
    for k in range(1, N):
        put(c_row.at[lax.rem(b + k, N)], r_cb.at[b], CB, over_b[k - 1])
    r_cb[b] = c_row[b]
    arrived(r_cb, CB)
    row = r_cb[0]
    for j in range(1, N):
        row = row + r_cb[j]
    c_one[0] = row
    r_cg[g] = row
    for k in range(1, N):
        put(c_one.at[0], r_cg.at[g], CG, over_g[k - 1])

    ld_ia.wait()
    arrived(r_p1, P1)
    swap_arrived(r_w, W)
    outer_wide = jnp.concatenate([r_w[j, 0] for j in range(N)], axis=1)
    mom_wide = jnp.concatenate([r_w[j, 1] for j in range(N)], axis=1)
    total = outer_wide - r_p1[0]
    for j in range(1, N):
        total = total + (outer_wide - r_p1[j])
    delta = total * (1.0 / N)
    for j in range(N):
        d_out[j] = delta[:, j * COLS : (j + 1) * COLS]
    swap(d_out, r_d, SW, 1)
    rp_out[0] = nesterov(outer_wide, mom_wide, delta)[0].astype(jnp.bfloat16)
    for k in range(1, N):
        put(rp_out.at[0], r_rp.at[g], RP, over_g[k - 1])
    r_rp[g] = rp_out[0]

    arrived(r_cg, CG)
    row = r_cg[0]
    for j in range(1, N):
        row = row + r_cg[j]
    row = row * (1.0 / N)
    c_fin[0] = row
    r_rb[b] = row
    for k in range(1, N):
        put(c_fin.at[0], r_rb.at[b], RB, over_b[k - 1])

    swap_arrived(r_d, SW)
    pack = jnp.concatenate([r_d[j] for j in range(N)], axis=1)
    d_pack[0] = pack
    r_ag[g] = pack
    for k in range(1, N):
        put(d_pack.at[0], r_ag.at[g], AG, over_g[k - 1])

    arrived(r_rb, RB)
    block = jnp.concatenate([r_rb[j] for j in range(N)], axis=0)
    c_blk[0] = block
    r_ra[a] = block
    for k in range(1, N):
        put(c_blk.at[0], r_ra.at[a], RA, over_a[k - 1])

    ld_in.wait()
    ld_on.wait()
    ld_mn.wait()
    arrived(r_norm, NR)
    outer_norm = v_on[...]
    total = outer_norm - r_norm[0]
    for j in range(1, N):
        total = total + (outer_norm - r_norm[j])
    o_n[...], o_mn[...] = nesterov(outer_norm, v_mn[...], total * (1.0 / N))
    outs = [load(o_n, new_n, L_NO), load(o_mn, new_mn, L_NO + 2)]

    ld_me.wait()
    arrived(r_ra, RA)
    change = jnp.dot(
        v_ba[...],
        r_ra[...].reshape(RANK, D),
        precision=HIGHEST,
        preferred_element_type=jnp.float32,
    ) * SCALE
    o_e[...], o_me[...] = nesterov(v_oe[...], v_me[...], change)
    outs += [load(o_e, new_e, L_IE), load(o_me, new_me, L_OE)]

    arrived(r_rp, RP)
    for j in range(N):
        o_rep[:, j * WIDE : (j + 1) * WIDE] = r_rp[j]
    outs += [load(o_rep, rep, L_RP)]
    arrived(r_ag, AG)
    for j in range(N):
        wide = r_ag[j]
        tall = jnp.concatenate(
            [wide[:, i * COLS : (i + 1) * COLS] for i in range(N)], axis=0
        )
        where = pl.ds(j * TALL, TALL)
        o_a[where, :], o_ma[where, :] = nesterov(v_oa[where, :], v_ma[where, :], tall)
    outs += [load(o_a, new_a, L_OA), load(o_ma, new_ma, L_MA)]

    for ref, phase in (
        (r_ca, CA), (r_cb, CB), (r_cg, CG), (r_rb, RB), (r_ra, RA), (r_p1, P1),
        (r_w, W), (r_norm, NR), (r_d, SW), (r_ag, AG), (r_rp, RP),
    ):
        whole(ref, phase, N - 1).wait_send()

    @pl.when(crossing)
    def _():
        for ref, turn in ((r_w, 0), (r_d, 1)):
            pltpu.make_async_remote_copy(
                src_ref=ref.at[0],
                dst_ref=ref.at[0],
                send_sem=once.at[turn],
                recv_sem=recv.at[W],
                device_id=over_g[0],
                device_id_type=MESH,
            ).wait_send()

    for copy in outs:
        copy.wait()


def on_device(*args):
    f32 = jnp.float32
    shapes = [
        ((240, D), f32), ((240, D), f32), ((D, COLS), f32), ((D, COLS), f32),
        ((4, ROWS), f32), ((4, ROWS), f32), ((ROWS, 4 * D), jnp.bfloat16),
    ]
    vmem = pltpu.VMEM
    return pl.pallas_call(
        kernel,
        out_shape=[jax.ShapeDtypeStruct(*shape) for shape in shapes],
        in_specs=[pl.BlockSpec(memory_space=pl.ANY)] * 10,
        out_specs=[pl.BlockSpec(memory_space=pl.ANY)] * 7,
        scratch_shapes=[
            vmem((240, D), f32), vmem((240, D), f32), vmem((240, D), f32),
            vmem((240, RANK), f32), vmem((D, COLS), f32), vmem((D, COLS), f32),
            vmem((4, ROWS), f32), vmem((4, ROWS), f32),
            vmem((N, 4, ROWS), f32),
            vmem((N, N, D), f32), vmem((N, N, D), f32),
            vmem((N, 1, D), f32), vmem((N, 1, D), f32),
            vmem((1, 1, D), f32), vmem((N, 1, D), f32),
            vmem((1, 1, D), f32), vmem((N, 1, D), f32),
            vmem((1, N, D), f32), vmem((N, N, D), f32),
            vmem((N, ROWS, WIDE), f32),
            vmem((N, 2, ROWS, COLS), f32), vmem((N, 2, ROWS, COLS), f32),
            vmem((N, ROWS, COLS), f32), vmem((N, ROWS, COLS), f32),
            vmem((1, ROWS, WIDE), f32), vmem((N, ROWS, WIDE), f32),
            vmem((1, ROWS, WIDE), jnp.bfloat16), vmem((N, ROWS, WIDE), jnp.bfloat16),
            *[vmem(*shape) for shape in shapes],
            pltpu.SemaphoreType.DMA((11,)), pltpu.SemaphoreType.DMA((11,)),
            pltpu.SemaphoreType.DMA((2,)), pltpu.SemaphoreType.DMA((16,)),
        ],
        compiler_params=pltpu.CompilerParams(
            collective_id=0, has_side_effects=True, vmem_limit_bytes=24 << 20
        ),
    )(*args)


def solution(mesh):
    return jax.shard_map(
        on_device,
        mesh=mesh,
        in_specs=(
            P("group", "shard", None),
            P("shard", None),
            P("shard", None),
            P("shard", None),
            P("group", "shard", None),
            P(None, "shard"),
            P(None, "shard"),
            P("group", None, "shard"),
            P(None, "shard"),
            P(None, "shard"),
        ),
        out_specs=(
            P("shard", None),
            P("shard", None),
            P(None, "shard"),
            P(None, "shard"),
            P(None, "shard"),
            P(None, "shard"),
            P("shard", None),
        ),
        check_vma=False,
    )
```

```python
import math

import jax
import jax.numpy as jnp
from jax import lax
from jax.experimental import pallas as pl
from jax.experimental.pallas import tpu as pltpu
from jax.sharding import PartitionSpec as P

VOCAB = 15360
RANK = 64
D = 768
N = 8
PLANE = 32
RING = 16
ROWS = 12
COLS = 48
WIDE = N * COLS
TALL = N * ROWS
PAIR = RANK // PLANE
MESH = pl.DeviceIdType.MESH
HIGHEST = lax.Precision.HIGHEST
SCALE = 1.0 / math.sqrt(RANK * VOCAB)
F32 = jnp.float32
BF16 = jnp.bfloat16

C1, CZ, C3, P1, W, NR, SW, AG, RP = range(9)
L_IE, L_OE, L_BA, L_OA, L_MA, L_IA, L_IN, L_ON = range(8)

G_STEPS = (4, 5, 3, 6, 2, 7, 1)
Z_STEPS = tuple(sorted(range(1, RING), key=lambda k: -min(k, RING - k)))
P_STEPS = tuple(
    sorted(
        [(i, j, k) for i in range(4) for j in range(4) for k in range(2)][1:],
        key=lambda t: -(min(t[0], 4 - t[0]) + min(t[1], 4 - t[1])),
    )
)


def nesterov(outer, moment, delta):
    moment_new = 0.5 * moment + delta
    return (outer - (delta + 0.5 * moment_new), moment_new)


def across(g, b):
    half, x = b // 4, lax.rem(b, 4)
    inner = jnp.logical_and(g >= 2, g <= 5)
    low = jnp.where(half == 0, g, 7 - g)
    outer_turn = jnp.where(low < 2, low, low - 4)
    turn = jnp.where(inner, g - 2, outer_turn)
    high, bit = turn // 2, lax.rem(turn, 2)
    x_high, x_bit = x // 2, lax.rem(x, 2)
    moved = 2 * lax.rem(x_high + high, 2) + lax.rem(x_bit + bit, 2)
    return (
        jnp.where(inner, g, 7 - g),
        4 * jnp.where(inner, half, 1 - half) + moved,
    )


def exchange(
    inner_e, outer_e, basis, inner_a, outer_a, mom_a, inner_n, outer_n,
    coef, delta_t, rep, norm,
    v_ie, v_oe, v_ba, v_oa, v_ma, v_on,
    c_part, r_c1, c_own, r_cz, c_fin, r_c3,
    r_p1, w_out, r_w, d_out, r_d, d_all, r_ag, rp_out, r_rp, r_norm,
    send, recv, once, local,
):
    g = lax.axis_index("group")
    s = lax.axis_index("shard")
    b, a = s // N, lax.rem(s, N)
    half, p = s // PLANE, lax.rem(s, PLANE)
    x, y, core = p // 8, lax.rem(p // 2, 4), lax.rem(p, 2)
    z = N * half + g
    far_g, far_b = across(g, b)

    def in_plane(step):
        i, j, k = step
        return 8 * lax.rem(x + i, 4) + 2 * lax.rem(y + j, 4) + lax.rem(core + k, 2)

    plane = [in_plane(step) for step in P_STEPS]
    ring = [lax.rem(z + k, RING) for k in Z_STEPS]
    line = [lax.rem(g + k, N) for k in G_STEPS]
    turns = [lax.rem(a + k, N) for k in range(N)]
    to_plane = [(g, PLANE * half + q) for q in plane]
    to_ring = [(lax.rem(q, N), PLANE * (q // N) + p) for q in ring]
    to_line = [(q, s) for q in line]
    to_swap = [(far_g, N * far_b + q) for q in turns]
    crossing = jnp.logical_or(far_b != b, far_g != g)

    def load(src, dst, sem):
        copy = pltpu.make_async_copy(src, dst, local.at[sem])
        copy.start()
        return copy

    def block(q):
        return inner_a.at[:, :, pl.ds(pl.multiple_of(q * WIDE, 128), WIDE)]

    ld_oa = load(outer_a, v_oa, L_OA)
    ld_ma = load(mom_a, v_ma, L_MA)
    ld_ie = load(inner_e.at[0], v_ie, L_IE)
    ld_oe = load(outer_e, v_oe, L_OE)
    ld_ba = load(basis, v_ba, L_BA)
    ld_ia = load(block(far_b), r_p1.at[g], L_IA)
    ld_in = load(inner_n.at[0], r_norm.at[g], L_IN)
    ld_on = load(outer_n, v_on, L_ON)

    barrier = pltpu.get_barrier_semaphore()

    def greet(device):
        pl.semaphore_signal(barrier, inc=1, device_id=device, device_id_type=MESH)

    for device in to_ring + to_plane + to_swap[1:]:
        greet(device)

    @pl.when(crossing)
    def _():
        greet(to_swap[0])

    def put(src, dst, phase, device, send_sem=None):
        pltpu.make_async_remote_copy(
            src_ref=src,
            dst_ref=dst,
            send_sem=send.at[phase] if send_sem is None else send_sem,
            recv_sem=recv.at[phase],
            device_id=device,
            device_id_type=MESH,
        ).start()

    def whole(ref, phase, count):
        part = ref.at[pl.ds(0, count)]
        return pltpu.make_async_remote_copy(
            src_ref=part,
            dst_ref=part,
            send_sem=send.at[phase],
            recv_sem=recv.at[phase],
            device_id=to_line[0],
            device_id_type=MESH,
        )

    def arrived(ref, phase):
        whole(ref, phase, ref.shape[0] - 1).wait_recv()

    def swap(src, dst, phase, turn):
        for k in range(1, N):
            put(src.at[turns[k]], dst.at[a], phase, to_swap[k])

        @pl.when(crossing)
        def _():
            put(src.at[a], dst.at[a], phase, to_swap[0], once.at[turn])

        @pl.when(jnp.logical_not(crossing))
        def _():
            dst[a] = src[a]

    def swap_arrived(ref, phase):
        @pl.when(crossing)
        def _():
            whole(ref, phase, N).wait_recv()

        @pl.when(jnp.logical_not(crossing))
        def _():
            whole(ref, phase, N - 1).wait_recv()

    ld_ie.wait()
    ld_oe.wait()
    ld_ba.wait()
    part = jnp.dot(
        v_ba[...],
        v_oe[...] - v_ie[...],
        precision=HIGHEST,
        preferred_element_type=F32,
    )
    for j in range(PLANE):
        c_part[j] = part[PAIR * j : PAIR * (j + 1), :]

    ld_oa.wait()
    ld_ma.wait()
    for i, ref in enumerate((v_oa, v_ma)):
        state = ref[...]
        rows = state[:, :TALL]
        for j in range(1, N):
            rows = jnp.where(far_b == j, state[:, TALL * j : TALL * (j + 1)], rows)
        rows = rows.T
        for j in range(N):
            w_out[j, i] = rows[ROWS * j : ROWS * (j + 1), :]

    pl.semaphore_wait(
        barrier, RING - 1 + PLANE - 1 + N - 1 + jnp.where(crossing, 1, 0)
    )

    for q, device in zip(plane, to_plane):
        put(c_part.at[q], r_c1.at[p], C1, device)
    for q, device in zip(line, to_line):
        put(block(across(q, b)[1]), r_p1.at[g], P1, device)
    swap(w_out, r_w, W, 0)
    for device in to_line:
        put(inner_n.at[0], r_norm.at[g], NR, device)

    r_c1[p] = c_part[p]
    arrived(r_c1, C1)
    row = r_c1[0]
    for j in range(1, PLANE):
        row = row + r_c1[j]
    c_own[0] = row
    for device in to_ring:
        put(c_own.at[0], r_cz.at[z], CZ, device)
    r_cz[z] = row

    swap_arrived(r_w, W)
    outer_wide = jnp.concatenate([r_w[j, 0] for j in range(N)], axis=1)
    mom_wide = jnp.concatenate([r_w[j, 1] for j in range(N)], axis=1)
    ld_ia.wait()
    arrived(r_p1, P1)
    total = outer_wide - r_p1[0, :, 0, :]
    for j in range(1, N):
        total = total + (outer_wide - r_p1[j, :, 0, :])
    delta = total * (1.0 / N)
    for j in range(N):
        d_out[j] = delta[:, COLS * j : COLS * (j + 1)]
    swap(d_out, r_d, SW, 1)
    replica = nesterov(outer_wide, mom_wide, delta)[0].astype(BF16)
    rp_out[0] = replica
    for device in to_line:
        put(rp_out.at[0], r_rp.at[far_b], RP, device)
    r_rp[far_b] = replica

    swap_arrived(r_d, SW)
    tall = jnp.concatenate([r_d[j] for j in range(N)], axis=0).T
    d_all[0] = tall
    for device in to_line:
        put(d_all.at[0], r_ag.at[far_b], AG, device)
    r_ag[far_b] = tall

    arrived(r_cz, CZ)
    row = r_cz[0]
    for j in range(1, RING):
        row = row + r_cz[j]
    row = row * (1.0 / N)
    c_fin[0] = row
    for device in to_plane:
        put(c_fin.at[0], r_c3.at[p], C3, device)
    r_c3[p] = row

    ld_in.wait()
    ld_on.wait()
    arrived(r_norm, NR)
    outer_norm = v_on[...]
    total = outer_norm - r_norm[0]
    for j in range(1, N):
        total = total + (outer_norm - r_norm[j])
    norm[...] = total * (1.0 / N)

    arrived(r_rp, RP)
    for j in range(N):
        rep[:, WIDE * j : WIDE * (j + 1)] = r_rp[j]
    arrived(r_c3, C3)
    for j in range(PLANE):
        coef[PAIR * j : PAIR * (j + 1), :] = r_c3[j]
    arrived(r_ag, AG)
    for j in range(N):
        delta_t[:, TALL * j : TALL * (j + 1)] = r_ag[j]

    for ref, phase in (
        (r_c1, C1), (r_cz, CZ), (r_c3, C3), (r_p1, P1), (r_norm, NR), (r_ag, AG),
        (r_rp, RP),
    ):
        whole(ref, phase, ref.shape[0] - 1).wait_send()
    for ref, phase in ((r_w, W), (r_d, SW)):
        whole(ref, phase, N - 1).wait_send()

    @pl.when(crossing)
    def _():
        for ref, turn in ((r_w, 0), (r_d, 1)):
            pltpu.make_async_remote_copy(
                src_ref=ref.at[0],
                dst_ref=ref.at[0],
                send_sem=once.at[turn],
                recv_sem=recv.at[W],
                device_id=to_line[0],
                device_id_type=MESH,
            ).wait_send()


def finish(
    coef, delta_t, rep, norm, outer_e, mom_e, basis, outer_a, mom_a, outer_n, mom_n,
    new_e, new_me, new_a, new_ma, new_n, new_mn, new_rep,
    o_e, o_me, o_a, o_ma, o_n, o_mn, sems,
):
    copies = []

    def store(src, dst):
        copy = pltpu.make_async_copy(src, dst, sems.at[len(copies)])
        copy.start()
        copies.append(copy)

    store(rep, new_rep)
    change = lax.dot_general(
        basis[...],
        coef[...],
        (((0,), (0,)), ((), ())),
        precision=HIGHEST,
        preferred_element_type=F32,
    ) * SCALE
    o_e[...], o_me[...] = nesterov(outer_e[...], mom_e[...], change)
    store(o_e, new_e)
    store(o_me, new_me)
    o_a[...], o_ma[...] = nesterov(outer_a[...], mom_a[...], delta_t[...])
    store(o_a, new_a)
    store(o_ma, new_ma)
    o_n[...], o_mn[...] = nesterov(outer_n[...], mom_n[...], norm[...])
    store(o_n, new_n)
    store(o_mn, new_mn)
    for copy in copies:
        copy.wait()


def on_device(
    inner_embed, outer_embed, moment_embed, basis, inner_attn, outer_attn,
    moment_attn, inner_norms, outer_norms, moment_norms,
):
    vmem = pltpu.VMEM
    dma = pltpu.SemaphoreType.DMA
    basis_t, outer_t, moment_t = basis.T, outer_attn.T, moment_attn.T
    inner_rows = inner_attn.reshape(ROWS, 1, 4 * D)
    in_place = pl.BlockSpec(memory_space=pl.ANY)
    on_chip = pl.BlockSpec(memory_space=pltpu.VMEM)
    shape = jax.ShapeDtypeStruct
    vocab = outer_embed.shape[0]

    coef, delta_t, rep, norm = pl.pallas_call(
        exchange,
        out_shape=[
            shape((RANK, D), F32), shape((COLS, D), F32),
            shape((ROWS, 4 * D), BF16), shape((4, ROWS), F32),
        ],
        in_specs=[in_place] * 8,
        out_specs=[on_chip] * 4,
        scratch_shapes=[
            vmem((vocab, D), F32), vmem((vocab, D), F32), vmem((RANK, vocab), F32),
            vmem((COLS, D), F32), vmem((COLS, D), F32), vmem((4, ROWS), F32),
            vmem((PLANE, PAIR, D), F32), vmem((PLANE, PAIR, D), F32),
            vmem((1, PAIR, D), F32), vmem((RING, PAIR, D), F32),
            vmem((1, PAIR, D), F32), vmem((PLANE, PAIR, D), F32),
            vmem((N, ROWS, 1, WIDE), F32),
            vmem((N, 2, ROWS, COLS), F32), vmem((N, 2, ROWS, COLS), F32),
            vmem((N, ROWS, COLS), F32), vmem((N, ROWS, COLS), F32),
            vmem((1, COLS, TALL), F32), vmem((N, COLS, TALL), F32),
            vmem((1, ROWS, WIDE), BF16), vmem((N, ROWS, WIDE), BF16),
            vmem((N, 4, ROWS), F32),
            dma((9,)), dma((9,)), dma((2,)), dma((8,)),
        ],
        compiler_params=pltpu.CompilerParams(
            collective_id=0, has_side_effects=True, vmem_limit_bytes=24 << 20
        ),
    )(
        inner_embed, outer_embed, basis_t, inner_rows, outer_t, moment_t,
        inner_norms, outer_norms,
    )

    outs = [
        shape((vocab, D), F32), shape((vocab, D), F32), shape((COLS, D), F32),
        shape((COLS, D), F32), shape((4, ROWS), F32), shape((4, ROWS), F32),
    ]
    new_e, new_me, new_a, new_ma, new_n, new_mn, replica = pl.pallas_call(
        finish,
        out_shape=[*outs, shape((ROWS, 4 * D), BF16)],
        in_specs=[on_chip] * 11,
        out_specs=[in_place] * 7,
        scratch_shapes=[*[vmem(out.shape, F32) for out in outs], dma((7,))],
        compiler_params=pltpu.CompilerParams(vmem_limit_bytes=16 << 20),
    )(
        coef, delta_t, rep, norm, outer_embed, moment_embed, basis_t, outer_t,
        moment_t, outer_norms, moment_norms,
    )
    return new_e, new_me, new_a.T, new_ma.T, new_n, new_mn, replica


def solution(mesh):
    return jax.shard_map(
        on_device,
        mesh=mesh,
        in_specs=(
            P("group", "shard", None),
            P("shard", None),
            P("shard", None),
            P("shard", None),
            P("group", "shard", None),
            P(None, "shard"),
            P(None, "shard"),
            P("group", None, "shard"),
            P(None, "shard"),
            P(None, "shard"),
        ),
        out_specs=(
            P("shard", None),
            P("shard", None),
            P(None, "shard"),
            P(None, "shard"),
            P(None, "shard"),
            P(None, "shard"),
            P("shard", None),
        ),
        check_vma=False,
    )
```

```python
import math

import jax
import jax.numpy as jnp
from jax import lax
from jax.experimental import pallas as pl
from jax.experimental.pallas import tpu as pltpu
from jax.sharding import PartitionSpec as P

VOCAB = 15360
RANK = 64
D = 768
N = 8
PLANE = 32
RING = 16
ROWS = 12
COLS = 48
WIDE = N * COLS
TALL = N * ROWS
PAIR = RANK // PLANE
MESH = pl.DeviceIdType.MESH
HIGHEST = lax.Precision.HIGHEST
SCALE = 1.0 / math.sqrt(RANK * VOCAB)
F32 = jnp.float32
BF16 = jnp.bfloat16

C1, CZ, C3, P1, W, NR, SW, AG, RP = range(9)
L_IE, L_OE, L_ME, L_BA, L_OA, L_MA, L_IA, L_IN, L_ON, L_MN = range(10)

G_STEPS = (4, 5, 3, 6, 2, 7, 1)
Z_STEPS = tuple(sorted(range(1, RING), key=lambda k: -min(k, RING - k)))
P_STEPS = tuple(
    sorted(
        [(i, j, k) for i in range(4) for j in range(4) for k in range(2)][1:],
        key=lambda t: -(min(t[0], 4 - t[0]) + min(t[1], 4 - t[1])),
    )
)


def nesterov(outer, moment, delta):
    moment_new = 0.5 * moment + delta
    return (outer - (delta + 0.5 * moment_new), moment_new)


def across(g, b):
    half, x = b // 4, lax.rem(b, 4)
    inner = jnp.logical_and(g >= 2, g <= 5)
    low = jnp.where(half == 0, g, 7 - g)
    outer_turn = jnp.where(low < 2, low, low - 4)
    turn = jnp.where(inner, g - 2, outer_turn)
    high, bit = turn // 2, lax.rem(turn, 2)
    x_high, x_bit = x // 2, lax.rem(x, 2)
    moved = 2 * lax.rem(x_high + high, 2) + lax.rem(x_bit + bit, 2)
    return (
        jnp.where(inner, g, 7 - g),
        4 * jnp.where(inner, half, 1 - half) + moved,
    )


def exchange(
    inner_e, outer_e, mom_e, basis, inner_a, outer_a, mom_a, inner_n, outer_n, mom_n,
    o_e, o_me, o_a, o_ma, o_n, o_mn, rep,
    v_ie, v_oe, v_me, v_ba, v_oa, v_ma, v_on, v_mn,
    c_part, r_c1, c_own, r_cz, c_fin, r_c3, coef,
    r_p1, w_out, r_w, d_out, r_d, d_all, r_ag, delta_t, rp_out, r_rp, r_norm,
    send, recv, once, local,
):
    g = lax.axis_index("group")
    s = lax.axis_index("shard")
    b, a = s // N, lax.rem(s, N)
    half, p = s // PLANE, lax.rem(s, PLANE)
    x, y, core = p // 8, lax.rem(p // 2, 4), lax.rem(p, 2)
    z = N * half + g
    far_g, far_b = across(g, b)

    def in_plane(step):
        i, j, k = step
        return 8 * lax.rem(x + i, 4) + 2 * lax.rem(y + j, 4) + lax.rem(core + k, 2)

    plane = [in_plane(step) for step in P_STEPS]
    ring = [lax.rem(z + k, RING) for k in Z_STEPS]
    line = [lax.rem(g + k, N) for k in G_STEPS]
    turns = [lax.rem(a + k, N) for k in range(N)]
    to_plane = [(g, PLANE * half + q) for q in plane]
    to_ring = [(lax.rem(q, N), PLANE * (q // N) + p) for q in ring]
    to_line = [(q, s) for q in line]
    to_swap = [(far_g, N * far_b + q) for q in turns]
    crossing = jnp.logical_or(far_b != b, far_g != g)

    barrier = pltpu.get_barrier_semaphore()

    def greet(device):
        pl.semaphore_signal(barrier, inc=1, device_id=device, device_id_type=MESH)

    for device in to_ring + to_plane + to_swap[1:]:
        greet(device)

    @pl.when(crossing)
    def _():
        greet(to_swap[0])

    def load(src, dst, sem):
        copy = pltpu.make_async_copy(src, dst, local.at[sem])
        copy.start()
        return copy

    def block(q):
        return inner_a.at[:, :, pl.ds(pl.multiple_of(q * WIDE, 128), WIDE)]

    ld_oa = load(outer_a, v_oa, L_OA)
    ld_ma = load(mom_a, v_ma, L_MA)
    ld_ie = load(inner_e.at[0], v_ie, L_IE)
    ld_oe = load(outer_e, v_oe, L_OE)
    ld_ba = load(basis, v_ba, L_BA)
    ld_ia = load(block(far_b), r_p1.at[g], L_IA)
    ld_in = load(inner_n.at[0], r_norm.at[g], L_IN)
    ld_on = load(outer_n, v_on, L_ON)
    ld_mn = load(mom_n, v_mn, L_MN)
    ld_me = load(mom_e, v_me, L_ME)

    def put(src, dst, phase, device, send_sem=None):
        pltpu.make_async_remote_copy(
            src_ref=src,
            dst_ref=dst,
            send_sem=send.at[phase] if send_sem is None else send_sem,
            recv_sem=recv.at[phase],
            device_id=device,
            device_id_type=MESH,
        ).start()

    def whole(ref, phase, count):
        part = ref.at[pl.ds(0, count)]
        return pltpu.make_async_remote_copy(
            src_ref=part,
            dst_ref=part,
            send_sem=send.at[phase],
            recv_sem=recv.at[phase],
            device_id=to_line[0],
            device_id_type=MESH,
        )

    def arrived(ref, phase):
        whole(ref, phase, ref.shape[0] - 1).wait_recv()

    def swap(src, dst, phase, turn):
        for k in range(1, N):
            put(src.at[turns[k]], dst.at[a], phase, to_swap[k])

        @pl.when(crossing)
        def _():
            put(src.at[a], dst.at[a], phase, to_swap[0], once.at[turn])

        @pl.when(jnp.logical_not(crossing))
        def _():
            dst[a] = src[a]

    def swap_arrived(ref, phase):
        @pl.when(crossing)
        def _():
            whole(ref, phase, N).wait_recv()

        @pl.when(jnp.logical_not(crossing))
        def _():
            whole(ref, phase, N - 1).wait_recv()

    pl.semaphore_wait(
        barrier, RING - 1 + PLANE - 1 + N - 1 + jnp.where(crossing, 1, 0)
    )

    for q, device in zip(line, to_line):
        put(block(across(q, b)[1]), r_p1.at[g], P1, device)

    ld_oa.wait()
    ld_ma.wait()
    for i, ref in enumerate((v_oa, v_ma)):
        state = ref[...]
        rows = state[:, :TALL]
        for j in range(1, N):
            rows = jnp.where(far_b == j, state[:, TALL * j : TALL * (j + 1)], rows)
        rows = rows.T
        for j in range(N):
            w_out[j, i] = rows[ROWS * j : ROWS * (j + 1), :]
    swap(w_out, r_w, W, 0)

    ld_ie.wait()
    ld_oe.wait()
    ld_ba.wait()
    part = jnp.dot(
        v_ba[...],
        v_oe[...] - v_ie[...],
        precision=HIGHEST,
        preferred_element_type=F32,
    )
    for j in range(PLANE):
        c_part[j] = part[PAIR * j : PAIR * (j + 1), :]
    for q, device in zip(plane, to_plane):
        put(c_part.at[q], r_c1.at[p], C1, device)
    r_c1[p] = c_part[p]
    for device in to_line:
        put(inner_n.at[0], r_norm.at[g], NR, device)

    swap_arrived(r_w, W)
    outer_wide = jnp.concatenate([r_w[j, 0] for j in range(N)], axis=1)
    mom_wide = jnp.concatenate([r_w[j, 1] for j in range(N)], axis=1)
    arrived(r_c1, C1)
    row = r_c1[0]
    for j in range(1, PLANE):
        row = row + r_c1[j]
    c_own[0] = row
    for device in to_ring:
        put(c_own.at[0], r_cz.at[z], CZ, device)
    r_cz[z] = row
    ld_ia.wait()
    arrived(r_p1, P1)
    total = outer_wide - r_p1[0, :, 0, :]
    for j in range(1, N):
        total = total + (outer_wide - r_p1[j, :, 0, :])
    delta = total * (1.0 / N)
    for j in range(N):
        d_out[j] = delta[:, COLS * j : COLS * (j + 1)]
    swap(d_out, r_d, SW, 1)
    replica = nesterov(outer_wide, mom_wide, delta)[0].astype(BF16)
    rp_out[0] = replica
    for device in to_line:
        put(rp_out.at[0], r_rp.at[far_b], RP, device)
    r_rp[far_b] = replica

    ld_in.wait()
    ld_on.wait()
    ld_mn.wait()
    arrived(r_norm, NR)
    outer_norm = v_on[...]
    total = outer_norm - r_norm[0]
    for j in range(1, N):
        total = total + (outer_norm - r_norm[j])
    o_n[...], o_mn[...] = nesterov(outer_norm, v_mn[...], total * (1.0 / N))

    swap_arrived(r_d, SW)
    tall = jnp.concatenate([r_d[j] for j in range(N)], axis=0).T
    d_all[0] = tall
    for device in to_line:
        put(d_all.at[0], r_ag.at[far_b], AG, device)
    r_ag[far_b] = tall

    arrived(r_cz, CZ)
    row = r_cz[0]
    for j in range(1, RING):
        row = row + r_cz[j]
    row = row * (1.0 / N)
    c_fin[0] = row
    for device in to_plane:
        put(c_fin.at[0], r_c3.at[p], C3, device)
    r_c3[p] = row

    arrived(r_rp, RP)
    for j in range(N):
        rep[:, WIDE * j : WIDE * (j + 1)] = r_rp[j]

    ld_me.wait()
    arrived(r_c3, C3)
    for j in range(PLANE):
        coef[PAIR * j : PAIR * (j + 1), :] = r_c3[j]
    change = lax.dot_general(
        v_ba[...],
        coef[...],
        (((0,), (0,)), ((), ())),
        precision=HIGHEST,
        preferred_element_type=F32,
    ) * SCALE
    o_e[...], o_me[...] = nesterov(v_oe[...], v_me[...], change)

    arrived(r_ag, AG)
    for j in range(N):
        delta_t[:, TALL * j : TALL * (j + 1)] = r_ag[j]
    o_a[...], o_ma[...] = nesterov(v_oa[...], v_ma[...], delta_t[...])

    for ref, phase in (
        (r_c1, C1), (r_cz, CZ), (r_c3, C3), (r_p1, P1), (r_norm, NR), (r_ag, AG),
        (r_rp, RP),
    ):
        whole(ref, phase, ref.shape[0] - 1).wait_send()
    for ref, phase in ((r_w, W), (r_d, SW)):
        whole(ref, phase, N - 1).wait_send()

    @pl.when(crossing)
    def _():
        for ref, turn in ((r_w, 0), (r_d, 1)):
            pltpu.make_async_remote_copy(
                src_ref=ref.at[0],
                dst_ref=ref.at[0],
                send_sem=once.at[turn],
                recv_sem=recv.at[W],
                device_id=to_line[0],
                device_id_type=MESH,
            ).wait_send()


def write(*refs):
    sems = refs[-1]
    copies = [
        pltpu.make_async_copy(refs[i], refs[7 + i], sems.at[i]) for i in range(7)
    ]
    for copy in copies:
        copy.start()
    for copy in copies:
        copy.wait()


def on_device(
    inner_embed, outer_embed, moment_embed, basis, inner_attn, outer_attn,
    moment_attn, inner_norms, outer_norms, moment_norms,
):
    vmem = pltpu.VMEM
    dma = pltpu.SemaphoreType.DMA
    basis_t, outer_t, moment_t = basis.T, outer_attn.T, moment_attn.T
    inner_rows = inner_attn.reshape(ROWS, 1, 4 * D)
    in_place = pl.BlockSpec(memory_space=pl.ANY)
    in_hbm = pl.BlockSpec(memory_space=pltpu.HBM)
    on_chip = pl.BlockSpec(memory_space=pltpu.VMEM)
    shape = jax.ShapeDtypeStruct
    vocab = outer_embed.shape[0]

    outs = [
        shape((vocab, D), F32), shape((vocab, D), F32), shape((COLS, D), F32),
        shape((COLS, D), F32), shape((4, ROWS), F32), shape((4, ROWS), F32),
        shape((ROWS, 4 * D), BF16),
    ]
    results = pl.pallas_call(
        exchange,
        out_shape=outs,
        in_specs=[in_hbm] * 10,
        out_specs=[on_chip] * 7,
        scratch_shapes=[
            vmem((vocab, D), F32), vmem((vocab, D), F32), vmem((vocab, D), F32),
            vmem((RANK, vocab), F32), vmem((COLS, D), F32), vmem((COLS, D), F32),
            vmem((4, ROWS), F32), vmem((4, ROWS), F32),
            vmem((PLANE, PAIR, D), F32), vmem((PLANE, PAIR, D), F32),
            vmem((1, PAIR, D), F32), vmem((RING, PAIR, D), F32),
            vmem((1, PAIR, D), F32), vmem((PLANE, PAIR, D), F32),
            vmem((RANK, D), F32),
            vmem((N, ROWS, 1, WIDE), F32),
            vmem((N, 2, ROWS, COLS), F32), vmem((N, 2, ROWS, COLS), F32),
            vmem((N, ROWS, COLS), F32), vmem((N, ROWS, COLS), F32),
            vmem((1, COLS, TALL), F32), vmem((N, COLS, TALL), F32),
            vmem((COLS, D), F32),
            vmem((1, ROWS, WIDE), BF16), vmem((N, ROWS, WIDE), BF16),
            vmem((N, 4, ROWS), F32),
            dma((9,)), dma((9,)), dma((2,)), dma((10,)),
        ],
        compiler_params=pltpu.CompilerParams(
            collective_id=0, has_side_effects=True, vmem_limit_bytes=24 << 20
        ),
    )(
        *[
            pltpu.with_memory_space_constraint(array, pltpu.HBM)
            for array in (
                inner_embed, outer_embed, moment_embed, basis_t, inner_rows, outer_t,
                moment_t, inner_norms, outer_norms, moment_norms,
            )
        ]
    )

    new_e, new_me, new_a, new_ma, new_n, new_mn, replica = pl.pallas_call(
        write,
        out_shape=outs,
        in_specs=[on_chip] * 7,
        out_specs=[in_place] * 7,
        scratch_shapes=[dma((7,))],
        compiler_params=pltpu.CompilerParams(vmem_limit_bytes=4 << 20),
    )(*results)
    return new_e, new_me, new_a.T, new_ma.T, new_n, new_mn, replica


def solution(mesh):
    return jax.shard_map(
        on_device,
        mesh=mesh,
        in_specs=(
            P("group", "shard", None),
            P("shard", None),
            P("shard", None),
            P("shard", None),
            P("group", "shard", None),
            P(None, "shard"),
            P(None, "shard"),
            P("group", None, "shard"),
            P(None, "shard"),
            P(None, "shard"),
        ),
        out_specs=(
            P("shard", None),
            P("shard", None),
            P(None, "shard"),
            P(None, "shard"),
            P(None, "shard"),
            P(None, "shard"),
            P("shard", None),
        ),
        check_vma=False,
    )
```

```python
import math

import jax
import jax.numpy as jnp
from jax import lax
from jax.experimental import pallas as pl
from jax.experimental.pallas import tpu as pltpu
from jax.sharding import PartitionSpec as P

VOCAB = 15360
RANK = 64
D = 768
N = 8
PLANE = 32
RING = 16
ROWS = 12
COLS = 48
WIDE = N * COLS
TALL = N * ROWS
PAIR = RANK // PLANE
MESH = pl.DeviceIdType.MESH
HIGHEST = lax.Precision.HIGHEST
SCALE = 1.0 / math.sqrt(RANK * VOCAB)
F32 = jnp.float32
BF16 = jnp.bfloat16

C1, CZ, C3, P1, W, NR, SW, S2, AG, RP = range(10)
L_IE, L_OE, L_ME, L_BA, L_OA, L_MA, L_IA, L_IN, L_ON, L_MN = range(10)

G_STEPS = (4, 5, 3, 6, 2, 7, 1)
Z_STEPS = tuple(sorted(range(1, RING), key=lambda k: -min(k, RING - k)))
P_STEPS = tuple(
    sorted(
        [(i, j, k) for i in range(4) for j in range(4) for k in range(2)][1:],
        key=lambda t: -(min(t[0], 4 - t[0]) + min(t[1], 4 - t[1])),
    )
)


def nesterov(outer, moment, delta):
    moment_new = 0.5 * moment + delta
    return (outer - (delta + 0.5 * moment_new), moment_new)


def inside(g):
    return jnp.logical_and(g >= 2, g <= 5)


def turned(g, half, x):
    low = jnp.where(half == 0, g, 7 - g)
    turn = jnp.where(inside(g), g - 2, jnp.where(low < 2, low, low - 4))
    high = lax.rem(x // 2 + turn // 2, 2)
    return 2 * high + lax.rem(lax.rem(x, 2) + lax.rem(turn, 2), 2)


def across(g, b):
    half, x = b // 4, lax.rem(b, 4)
    to_half = jnp.where(inside(g), half, 1 - half)
    return jnp.where(inside(g), g, 7 - g), 4 * to_half + turned(g, half, x)


def second(g):
    return jnp.where(
        inside(g), lax.rem(g + 4, N), jnp.where(g < 4, g + 2, g - 2)
    )


def second_from(g, b):
    half, x = b // 4, lax.rem(b, 4)
    owner = jnp.where(
        inside(g), jnp.where(g < 4, g - 2, g + 2), lax.rem(g + 4, N)
    )
    from_half = jnp.where(inside(owner), half, 1 - half)
    return owner, 4 * from_half + turned(owner, from_half, x)


def exchange(
    inner_e, outer_e, mom_e, basis, inner_a, outer_a, mom_a, inner_n, outer_n, mom_n,
    o_e, o_me, o_a, o_ma, o_n, o_mn, rep,
    v_ie, v_oe, v_me, v_ba, v_oa, v_ma, v_on, v_mn,
    c_part, r_c1, c_own, r_cz, c_fin, r_c3, coef,
    r_p1, w_out, r_w, d_out, r_d, r_d2, d_all, r_ag, delta_t, rp_out, r_rp, r_norm,
    send, recv, once, local,
):
    g = lax.axis_index("group")
    s = lax.axis_index("shard")
    b, a = s // N, lax.rem(s, N)
    half, p = s // PLANE, lax.rem(s, PLANE)
    x, y, core = p // 8, lax.rem(p // 2, 4), lax.rem(p, 2)
    z = N * half + g
    far_g, far_b = across(g, b)
    from_g, from_b = second_from(g, b)

    def in_plane(step):
        i, j, k = step
        return 8 * lax.rem(x + i, 4) + 2 * lax.rem(y + j, 4) + lax.rem(core + k, 2)

    plane = [in_plane(step) for step in P_STEPS]
    ring = [lax.rem(z + k, RING) for k in Z_STEPS]
    line = [lax.rem(g + k, N) for k in G_STEPS]
    turns = [lax.rem(a + k, N) for k in range(N)]
    to_plane = [(g, PLANE * half + q) for q in plane]
    to_ring = [(lax.rem(q, N), PLANE * (q // N) + p) for q in ring]
    to_line = [(q, s) for q in line]
    to_swap = [(far_g, N * far_b + q) for q in turns]
    to_second = [(second(g), N * far_b + q) for q in turns]
    to_near = [
        (4 * (g // 4) + lax.rem(g + k, 4), s) for k in (2, 1, 3)
    ]
    crossing = jnp.logical_or(far_b != b, far_g != g)

    barrier = pltpu.get_barrier_semaphore()

    def greet(device):
        pl.semaphore_signal(barrier, inc=1, device_id=device, device_id_type=MESH)

    for device in to_ring + to_swap[1:] + to_plane:
        greet(device)

    @pl.when(crossing)
    def _():
        greet(to_swap[0])

    def load(src, dst, sem):
        copy = pltpu.make_async_copy(src, dst, local.at[sem])
        copy.start()
        return copy

    def block(q):
        return inner_a.at[:, :, pl.ds(pl.multiple_of(q * WIDE, 128), WIDE)]

    ld_oa = load(outer_a, v_oa, L_OA)
    ld_ma = load(mom_a, v_ma, L_MA)
    ld_ie = load(inner_e.at[0], v_ie, L_IE)
    ld_oe = load(outer_e, v_oe, L_OE)
    ld_ba = load(basis, v_ba, L_BA)
    ld_ia = load(block(far_b), r_p1.at[g], L_IA)
    ld_in = load(inner_n.at[0], r_norm.at[g], L_IN)
    ld_on = load(outer_n, v_on, L_ON)
    ld_mn = load(mom_n, v_mn, L_MN)
    ld_me = load(mom_e, v_me, L_ME)

    def put(src, dst, phase, device, send_sem=None):
        pltpu.make_async_remote_copy(
            src_ref=src,
            dst_ref=dst,
            send_sem=send.at[phase] if send_sem is None else send_sem,
            recv_sem=recv.at[phase],
            device_id=device,
            device_id_type=MESH,
        ).start()

    def whole(ref, phase, count):
        part = ref.at[pl.ds(0, count)]
        return pltpu.make_async_remote_copy(
            src_ref=part,
            dst_ref=part,
            send_sem=send.at[phase],
            recv_sem=recv.at[phase],
            device_id=to_line[0],
            device_id_type=MESH,
        )

    def arrived(ref, phase):
        whole(ref, phase, ref.shape[0] - 1).wait_recv()

    def swap(src, dst, phase, turn):
        for k in range(1, N):
            put(src.at[turns[k]], dst.at[a], phase, to_swap[k])

        @pl.when(crossing)
        def _():
            put(src.at[a], dst.at[a], phase, to_swap[0], once.at[turn])

        @pl.when(jnp.logical_not(crossing))
        def _():
            dst[a] = src[a]

    def swap_arrived(ref, phase):
        @pl.when(crossing)
        def _():
            whole(ref, phase, N).wait_recv()

        @pl.when(jnp.logical_not(crossing))
        def _():
            whole(ref, phase, N - 1).wait_recv()

    pl.semaphore_wait(
        barrier, RING - 1 + PLANE - 1 + N - 1 + jnp.where(crossing, 1, 0)
    )

    for q, device in zip(line, to_line):
        put(block(across(q, b)[1]), r_p1.at[g], P1, device)

    ld_oa.wait()
    ld_ma.wait()
    for i, ref in enumerate((v_oa, v_ma)):
        state = ref[...]
        rows = state[:, :TALL]
        for j in range(1, N):
            rows = jnp.where(far_b == j, state[:, TALL * j : TALL * (j + 1)], rows)
        rows = rows.T
        for j in range(N):
            w_out[j, i] = rows[ROWS * j : ROWS * (j + 1), :]
    swap(w_out, r_w, W, 0)

    ld_ie.wait()
    ld_oe.wait()
    ld_ba.wait()
    part = jnp.dot(
        v_ba[...],
        v_oe[...] - v_ie[...],
        precision=HIGHEST,
        preferred_element_type=F32,
    )
    for j in range(PLANE):
        c_part[j] = part[PAIR * j : PAIR * (j + 1), :]
    for q, device in zip(plane, to_plane):
        put(c_part.at[q], r_c1.at[p], C1, device)
    r_c1[p] = c_part[p]
    for device in to_line:
        put(inner_n.at[0], r_norm.at[g], NR, device)

    swap_arrived(r_w, W)
    outer_wide = jnp.concatenate([r_w[j, 0] for j in range(N)], axis=1)
    mom_wide = jnp.concatenate([r_w[j, 1] for j in range(N)], axis=1)
    arrived(r_c1, C1)
    row = r_c1[0]
    for j in range(1, PLANE):
        row = row + r_c1[j]
    c_own[0] = row
    for device in to_ring:
        put(c_own.at[0], r_cz.at[z], CZ, device)
    r_cz[z] = row
    ld_ia.wait()
    arrived(r_p1, P1)
    total = outer_wide - r_p1[0, :, 0, :]
    for j in range(1, N):
        total = total + (outer_wide - r_p1[j, :, 0, :])
    delta = total * (1.0 / N)
    for j in range(N):
        chunk = delta[:, COLS * j : COLS * (j + 1)]
        d_out[j] = jnp.concatenate(
            [chunk[: ROWS // 2, :], chunk[ROWS // 2 :, :]], axis=1
        )
    for k in range(N):
        put(d_out.at[turns[k]], r_d2.at[a], S2, to_second[k])
    swap(d_out, r_d, SW, 1)
    replica = nesterov(outer_wide, mom_wide, delta)[0].astype(BF16)
    rp_out[0] = replica
    for device in to_line:
        put(rp_out.at[0], r_rp.at[far_b], RP, device)
    r_rp[far_b] = replica

    ld_in.wait()
    ld_on.wait()
    ld_mn.wait()
    arrived(r_norm, NR)
    outer_norm = v_on[...]
    total = outer_norm - r_norm[0]
    for j in range(1, N):
        total = total + (outer_norm - r_norm[j])
    o_n[...], o_mn[...] = nesterov(outer_norm, v_mn[...], total * (1.0 / N))

    def gather(ref, turn, rows):
        parts = []
        for j in range(N):
            parts += [ref[j, :, :COLS], ref[j, :, COLS:]]
        tall = jnp.concatenate(parts, axis=0).T
        d_all[turn] = tall
        for device in to_near:
            put(d_all.at[turn], r_ag.at[rows], AG, device)
        r_ag[rows] = tall

    swap_arrived(r_d, SW)
    gather(r_d, 0, far_b)

    arrived(r_cz, CZ)
    row = r_cz[0]
    for j in range(1, RING):
        row = row + r_cz[j]
    row = row * (1.0 / N)
    c_fin[0] = row
    for device in to_plane:
        put(c_fin.at[0], r_c3.at[p], C3, device)
    r_c3[p] = row

    whole(r_d2, S2, N).wait_recv()
    gather(r_d2, 1, from_b)

    arrived(r_rp, RP)
    for j in range(N):
        rep[:, WIDE * j : WIDE * (j + 1)] = r_rp[j]

    ld_me.wait()
    arrived(r_c3, C3)
    for j in range(PLANE):
        coef[PAIR * j : PAIR * (j + 1), :] = r_c3[j]
    change = lax.dot_general(
        v_ba[...],
        coef[...],
        (((0,), (0,)), ((), ())),
        precision=HIGHEST,
        preferred_element_type=F32,
    ) * SCALE
    o_e[...], o_me[...] = nesterov(v_oe[...], v_me[...], change)

    whole(r_ag, AG, 6).wait_recv()
    for j in range(N):
        delta_t[:, TALL * j : TALL * (j + 1)] = r_ag[j]
    o_a[...], o_ma[...] = nesterov(v_oa[...], v_ma[...], delta_t[...])

    for ref, phase in (
        (r_c1, C1), (r_cz, CZ), (r_c3, C3), (r_p1, P1), (r_norm, NR), (r_rp, RP),
    ):
        whole(ref, phase, ref.shape[0] - 1).wait_send()
    for ref, phase, count in ((r_w, W, N - 1), (r_d, SW, N - 1), (r_d2, S2, N), (r_ag, AG, 6)):
        whole(ref, phase, count).wait_send()

    @pl.when(crossing)
    def _():
        for ref, turn in ((r_w, 0), (r_d, 1)):
            pltpu.make_async_remote_copy(
                src_ref=ref.at[0],
                dst_ref=ref.at[0],
                send_sem=once.at[turn],
                recv_sem=recv.at[W],
                device_id=to_line[0],
                device_id_type=MESH,
            ).wait_send()


def write(*refs):
    sems = refs[-1]
    copies = [
        pltpu.make_async_copy(refs[i], refs[7 + i], sems.at[i]) for i in range(7)
    ]
    for copy in copies:
        copy.start()
    for copy in copies:
        copy.wait()


def on_device(
    inner_embed, outer_embed, moment_embed, basis, inner_attn, outer_attn,
    moment_attn, inner_norms, outer_norms, moment_norms,
):
    vmem = pltpu.VMEM
    dma = pltpu.SemaphoreType.DMA
    basis_t, outer_t, moment_t = basis.T, outer_attn.T, moment_attn.T
    inner_rows = inner_attn.reshape(ROWS, 1, 4 * D)
    in_place = pl.BlockSpec(memory_space=pl.ANY)
    in_hbm = pl.BlockSpec(memory_space=pltpu.HBM)
    on_chip = pl.BlockSpec(memory_space=pltpu.VMEM)
    shape = jax.ShapeDtypeStruct
    vocab = outer_embed.shape[0]

    outs = [
        shape((vocab, D), F32), shape((vocab, D), F32), shape((COLS, D), F32),
        shape((COLS, D), F32), shape((4, ROWS), F32), shape((4, ROWS), F32),
        shape((ROWS, 4 * D), BF16),
    ]
    results = pl.pallas_call(
        exchange,
        out_shape=outs,
        in_specs=[in_hbm] * 10,
        out_specs=[on_chip] * 7,
        scratch_shapes=[
            vmem((vocab, D), F32), vmem((vocab, D), F32), vmem((vocab, D), F32),
            vmem((RANK, vocab), F32), vmem((COLS, D), F32), vmem((COLS, D), F32),
            vmem((4, ROWS), F32), vmem((4, ROWS), F32),
            vmem((PLANE, PAIR, D), F32), vmem((PLANE, PAIR, D), F32),
            vmem((1, PAIR, D), F32), vmem((RING, PAIR, D), F32),
            vmem((1, PAIR, D), F32), vmem((PLANE, PAIR, D), F32),
            vmem((RANK, D), F32),
            vmem((N, ROWS, 1, WIDE), F32),
            vmem((N, 2, ROWS, COLS), F32), vmem((N, 2, ROWS, COLS), F32),
            vmem((N, ROWS // 2, 2 * COLS), F32), vmem((N, ROWS // 2, 2 * COLS), F32),
            vmem((N, ROWS // 2, 2 * COLS), F32),
            vmem((2, COLS, TALL), F32), vmem((N, COLS, TALL), F32),
            vmem((COLS, D), F32),
            vmem((1, ROWS, WIDE), BF16), vmem((N, ROWS, WIDE), BF16),
            vmem((N, 4, ROWS), F32),
            dma((10,)), dma((10,)), dma((2,)), dma((10,)),
        ],
        compiler_params=pltpu.CompilerParams(
            collective_id=0, has_side_effects=True, vmem_limit_bytes=24 << 20
        ),
    )(
        *[
            pltpu.with_memory_space_constraint(array, pltpu.HBM)
            for array in (
                inner_embed, outer_embed, moment_embed, basis_t, inner_rows, outer_t,
                moment_t, inner_norms, outer_norms, moment_norms,
            )
        ]
    )

    new_e, new_me, new_a, new_ma, new_n, new_mn, replica = pl.pallas_call(
        write,
        out_shape=outs,
        in_specs=[on_chip] * 7,
        out_specs=[in_place] * 7,
        scratch_shapes=[dma((7,))],
        compiler_params=pltpu.CompilerParams(vmem_limit_bytes=4 << 20),
    )(*results)
    return new_e, new_me, new_a.T, new_ma.T, new_n, new_mn, replica


def solution(mesh):
    return jax.shard_map(
        on_device,
        mesh=mesh,
        in_specs=(
            P("group", "shard", None),
            P("shard", None),
            P("shard", None),
            P("shard", None),
            P("group", "shard", None),
            P(None, "shard"),
            P(None, "shard"),
            P("group", None, "shard"),
            P(None, "shard"),
            P(None, "shard"),
        ),
        out_specs=(
            P("shard", None),
            P("shard", None),
            P(None, "shard"),
            P(None, "shard"),
            P(None, "shard"),
            P(None, "shard"),
            P("shard", None),
        ),
        check_vma=False,
    )
```

```python
import math

import jax
import jax.numpy as jnp
from jax import lax
from jax.experimental import pallas as pl
from jax.experimental.pallas import tpu as pltpu
from jax.sharding import PartitionSpec as P

VOCAB = 15360
RANK = 64
D = 768
N = 8
PLANE = 32
RING = 16
ROWS = 12
COLS = 48
WIDE = N * COLS
TALL = N * ROWS
LEFT = 36
PAIR = RANK // PLANE
MESH = pl.DeviceIdType.MESH
HIGHEST = lax.Precision.HIGHEST
SCALE = 1.0 / math.sqrt(RANK * VOCAB)
F32 = jnp.float32
BF16 = jnp.bfloat16

C1, CZ, C3, P1, W, NR, SW, S2, AG, RP = range(10)
L_IE, L_OE, L_ME, L_BA, L_OA, L_MA, L_IA, L_IN, L_ON, L_MN = range(10)

G_STEPS = (4, 5, 3, 6, 2, 7, 1)
Z_STEPS = tuple(sorted(range(1, RING), key=lambda k: -min(k, RING - k)))
P_STEPS = tuple(
    sorted(
        [(i, j, k) for i in range(4) for j in range(4) for k in range(2)][1:],
        key=lambda t: -(min(t[0], 4 - t[0]) + min(t[1], 4 - t[1])),
    )
)


def nesterov(outer, moment, delta):
    moment_new = 0.5 * moment + delta
    return (outer - (delta + 0.5 * moment_new), moment_new)


def inside(g):
    return jnp.logical_and(g >= 2, g <= 5)


def turned(g, half, x):
    low = jnp.where(half == 0, g, 7 - g)
    turn = jnp.where(inside(g), g - 2, jnp.where(low < 2, low, low - 4))
    high = lax.rem(x // 2 + turn // 2, 2)
    return 2 * high + lax.rem(lax.rem(x, 2) + lax.rem(turn, 2), 2)


def across(g, b):
    half, x = b // 4, lax.rem(b, 4)
    to_half = jnp.where(inside(g), half, 1 - half)
    return jnp.where(inside(g), g, 7 - g), 4 * to_half + turned(g, half, x)


def second(g):
    return jnp.where(
        inside(g), lax.rem(g + 4, N), jnp.where(g < 4, g + 2, g - 2)
    )


def second_from(g, b):
    half, x = b // 4, lax.rem(b, 4)
    owner = jnp.where(
        inside(g), jnp.where(g < 4, g - 2, g + 2), lax.rem(g + 4, N)
    )
    from_half = jnp.where(inside(owner), half, 1 - half)
    return owner, 4 * from_half + turned(owner, from_half, x)


def exchange(
    inner_e, outer_e, mom_e, basis, inner_a, outer_a, mom_a, inner_n, outer_n, mom_n,
    o_e, o_me, o_a, o_ma, o_n, o_mn, rep,
    v_ie, v_oe, v_me, v_ba, v_oa, v_ma, v_on, v_mn,
    c_part, r_c1, c_own, r_cz, c_fin, r_c3, coef,
    r_p1, w_out, r_w, d_out, r_d, r_d2, d_all, r_ag, delta_t, rp_out, r_rp, r_norm,
    send, recv, once, local,
):
    g = lax.axis_index("group")
    s = lax.axis_index("shard")
    b, a = s // N, lax.rem(s, N)
    half, p = s // PLANE, lax.rem(s, PLANE)
    x, y, core = p // 8, lax.rem(p // 2, 4), lax.rem(p, 2)
    z = N * half + g
    far_g, far_b = across(g, b)
    from_g, from_b = second_from(g, b)

    def in_plane(step):
        i, j, k = step
        return 8 * lax.rem(x + i, 4) + 2 * lax.rem(y + j, 4) + lax.rem(core + k, 2)

    plane = [in_plane(step) for step in P_STEPS]
    ring = [lax.rem(z + k, RING) for k in Z_STEPS]
    line = [lax.rem(g + k, N) for k in G_STEPS]
    turns = [lax.rem(a + k, N) for k in range(N)]
    to_plane = [(g, PLANE * half + q) for q in plane]
    to_ring = [(lax.rem(q, N), PLANE * (q // N) + p) for q in ring]
    to_line = [(q, s) for q in line]
    to_swap = [(far_g, N * far_b + q) for q in turns]
    to_second = [(second(g), N * far_b + q) for q in turns]
    turn_first = jnp.where(lax.rem(g, 4) < 2, 3, 1)
    to_near = [
        (4 * (g // 4) + lax.rem(g + k, 4), s) for k in (turn_first, 2, 4 - turn_first)
    ]
    crossing = jnp.logical_or(far_b != b, far_g != g)

    barrier = pltpu.get_barrier_semaphore()

    def greet(device):
        pl.semaphore_signal(barrier, inc=1, device_id=device, device_id_type=MESH)

    for device in to_ring + to_swap[1:] + to_plane:
        greet(device)

    @pl.when(crossing)
    def _():
        greet(to_swap[0])

    def load(src, dst, sem):
        copy = pltpu.make_async_copy(src, dst, local.at[sem])
        copy.start()
        return copy

    def block(q):
        return inner_a.at[:, :, pl.ds(pl.multiple_of(q * WIDE, 128), WIDE)]

    ld_oa = load(outer_a, v_oa, L_OA)
    ld_ma = load(mom_a, v_ma, L_MA)
    ld_ie = load(inner_e.at[0], v_ie, L_IE)
    ld_oe = load(outer_e, v_oe, L_OE)
    ld_ba = load(basis, v_ba, L_BA)
    ld_ia = load(block(far_b), r_p1.at[g], L_IA)
    ld_in = load(inner_n.at[0], r_norm.at[g], L_IN)
    ld_on = load(outer_n, v_on, L_ON)
    ld_mn = load(mom_n, v_mn, L_MN)
    ld_me = load(mom_e, v_me, L_ME)

    def put(src, dst, phase, device, send_sem=None):
        pltpu.make_async_remote_copy(
            src_ref=src,
            dst_ref=dst,
            send_sem=send.at[phase] if send_sem is None else send_sem,
            recv_sem=recv.at[phase],
            device_id=device,
            device_id_type=MESH,
        ).start()

    def whole(ref, phase, count):
        part = ref.at[pl.ds(0, count)]
        return pltpu.make_async_remote_copy(
            src_ref=part,
            dst_ref=part,
            send_sem=send.at[phase],
            recv_sem=recv.at[phase],
            device_id=to_line[0],
            device_id_type=MESH,
        )

    def arrived(ref, phase):
        whole(ref, phase, ref.shape[0] - 1).wait_recv()

    def swap(src, dst, phase, turn):
        for k in range(1, N):
            put(src.at[turns[k]], dst.at[a], phase, to_swap[k])

        @pl.when(crossing)
        def _():
            put(src.at[a], dst.at[a], phase, to_swap[0], once.at[turn])

        @pl.when(jnp.logical_not(crossing))
        def _():
            dst[a] = src[a]

    def swap_arrived(ref, phase):
        @pl.when(crossing)
        def _():
            whole(ref, phase, N).wait_recv()

        @pl.when(jnp.logical_not(crossing))
        def _():
            whole(ref, phase, N - 1).wait_recv()

    pl.semaphore_wait(
        barrier, RING - 1 + PLANE - 1 + N - 1 + jnp.where(crossing, 1, 0)
    )

    for q, device in zip(line, to_line):
        put(block(across(q, b)[1]), r_p1.at[g], P1, device)

    ld_oa.wait()
    ld_ma.wait()
    for i, ref in enumerate((v_oa, v_ma)):
        state = ref[...]
        rows = state[:, :TALL]
        for j in range(1, N):
            rows = jnp.where(far_b == j, state[:, TALL * j : TALL * (j + 1)], rows)
        rows = rows.T
        for j in range(N):
            w_out[j, i] = rows[ROWS * j : ROWS * (j + 1), :]
    swap(w_out, r_w, W, 0)

    ld_ie.wait()
    ld_oe.wait()
    ld_ba.wait()
    part = jnp.dot(
        v_ba[...],
        v_oe[...] - v_ie[...],
        precision=HIGHEST,
        preferred_element_type=F32,
    )
    for j in range(PLANE):
        c_part[j] = part[PAIR * j : PAIR * (j + 1), :]
    for q, device in zip(plane, to_plane):
        put(c_part.at[q], r_c1.at[p], C1, device)
    r_c1[p] = c_part[p]
    for device in to_line:
        put(inner_n.at[0], r_norm.at[g], NR, device)

    swap_arrived(r_w, W)
    outer_wide = jnp.concatenate([r_w[j, 0] for j in range(N)], axis=1)
    mom_wide = jnp.concatenate([r_w[j, 1] for j in range(N)], axis=1)
    arrived(r_c1, C1)
    row = r_c1[0]
    for j in range(1, PLANE):
        row = row + r_c1[j]
    c_own[0] = row
    for device in to_ring:
        put(c_own.at[0], r_cz.at[z], CZ, device)
    r_cz[z] = row
    ld_ia.wait()
    arrived(r_p1, P1)
    total = outer_wide - r_p1[0, :, 0, :]
    for j in range(1, N):
        total = total + (outer_wide - r_p1[j, :, 0, :])
    delta = total * (1.0 / N)
    for j in range(N):
        chunk = delta[:, COLS * j : COLS * (j + 1)]
        d_out[j] = jnp.concatenate(
            [chunk[: ROWS // 2, :], chunk[ROWS // 2 :, :]], axis=1
        )
    for k in range(N):
        put(d_out.at[turns[k]], r_d2.at[a], S2, to_second[k])
    swap(d_out, r_d, SW, 1)
    replica = nesterov(outer_wide, mom_wide, delta)[0].astype(BF16)
    rp_out[0] = replica
    for device in to_line:
        put(rp_out.at[0], r_rp.at[far_b], RP, device)
    r_rp[far_b] = replica

    ld_in.wait()
    ld_on.wait()
    ld_mn.wait()
    arrived(r_norm, NR)
    outer_norm = v_on[...]
    total = outer_norm - r_norm[0]
    for j in range(1, N):
        total = total + (outer_norm - r_norm[j])
    o_n[...], o_mn[...] = nesterov(outer_norm, v_mn[...], total * (1.0 / N))

    def gather(ref, turn, rows):
        parts = []
        for j in range(N):
            parts += [ref[j, :, :COLS], ref[j, :, COLS:]]
        tall = jnp.concatenate(parts, axis=0).T
        rest = [tall[LEFT:, 32 * j : 32 * (j + 1)] for j in range(3)]
        tall = jnp.concatenate(
            [tall[:LEFT, :], jnp.concatenate(rest, axis=0)], axis=1
        )
        d_all[turn] = tall
        for device in to_near:
            put(d_all.at[turn], r_ag.at[rows], AG, device)
        r_ag[rows] = tall


    arrived(r_cz, CZ)
    row = r_cz[0]
    for j in range(1, RING):
        row = row + r_cz[j]
    row = row * (1.0 / N)
    c_fin[0] = row
    for device in to_plane:
        put(c_fin.at[0], r_c3.at[p], C3, device)
    r_c3[p] = row

    swap_arrived(r_d, SW)
    gather(r_d, 0, far_b)
    whole(r_d2, S2, N).wait_recv()
    gather(r_d2, 1, from_b)

    arrived(r_rp, RP)
    for j in range(N):
        rep[:, WIDE * j : WIDE * (j + 1)] = r_rp[j]

    ld_me.wait()
    arrived(r_c3, C3)
    for j in range(PLANE):
        coef[PAIR * j : PAIR * (j + 1), :] = r_c3[j]
    change = lax.dot_general(
        v_ba[...],
        coef[...],
        (((0,), (0,)), ((), ())),
        precision=HIGHEST,
        preferred_element_type=F32,
    ) * SCALE
    o_e[...], o_me[...] = nesterov(v_oe[...], v_me[...], change)

    whole(r_ag, AG, 6).wait_recv()
    for j in range(N):
        packed = r_ag[j]
        rest = [packed[12 * i : 12 * (i + 1), TALL:] for i in range(3)]
        delta_t[:LEFT, TALL * j : TALL * (j + 1)] = packed[:, :TALL]
        delta_t[LEFT:, TALL * j : TALL * (j + 1)] = jnp.concatenate(rest, axis=1)
    o_a[...], o_ma[...] = nesterov(v_oa[...], v_ma[...], delta_t[...])

    for ref, phase in (
        (r_c1, C1), (r_cz, CZ), (r_c3, C3), (r_p1, P1), (r_norm, NR), (r_rp, RP),
    ):
        whole(ref, phase, ref.shape[0] - 1).wait_send()
    for ref, phase, count in ((r_w, W, N - 1), (r_d, SW, N - 1), (r_d2, S2, N), (r_ag, AG, 6)):
        whole(ref, phase, count).wait_send()

    @pl.when(crossing)
    def _():
        for ref, turn in ((r_w, 0), (r_d, 1)):
            pltpu.make_async_remote_copy(
                src_ref=ref.at[0],
                dst_ref=ref.at[0],
                send_sem=once.at[turn],
                recv_sem=recv.at[W],
                device_id=to_line[0],
                device_id_type=MESH,
            ).wait_send()


def write(*refs):
    sems = refs[-1]
    copies = [
        pltpu.make_async_copy(refs[i], refs[7 + i], sems.at[i]) for i in range(7)
    ]
    for copy in copies:
        copy.start()
    for copy in copies:
        copy.wait()


def on_device(
    inner_embed, outer_embed, moment_embed, basis, inner_attn, outer_attn,
    moment_attn, inner_norms, outer_norms, moment_norms,
):
    vmem = pltpu.VMEM
    dma = pltpu.SemaphoreType.DMA
    basis_t, outer_t, moment_t = basis.T, outer_attn.T, moment_attn.T
    inner_rows = inner_attn.reshape(ROWS, 1, 4 * D)
    in_place = pl.BlockSpec(memory_space=pl.ANY)
    in_hbm = pl.BlockSpec(memory_space=pltpu.HBM)
    on_chip = pl.BlockSpec(memory_space=pltpu.VMEM)
    shape = jax.ShapeDtypeStruct
    vocab = outer_embed.shape[0]

    outs = [
        shape((vocab, D), F32), shape((vocab, D), F32), shape((COLS, D), F32),
        shape((COLS, D), F32), shape((4, ROWS), F32), shape((4, ROWS), F32),
        shape((ROWS, 4 * D), BF16),
    ]
    results = pl.pallas_call(
        exchange,
        out_shape=outs,
        in_specs=[in_hbm] * 10,
        out_specs=[on_chip] * 7,
        scratch_shapes=[
            vmem((vocab, D), F32), vmem((vocab, D), F32), vmem((vocab, D), F32),
            vmem((RANK, vocab), F32), vmem((COLS, D), F32), vmem((COLS, D), F32),
            vmem((4, ROWS), F32), vmem((4, ROWS), F32),
            vmem((PLANE, PAIR, D), F32), vmem((PLANE, PAIR, D), F32),
            vmem((1, PAIR, D), F32), vmem((RING, PAIR, D), F32),
            vmem((1, PAIR, D), F32), vmem((PLANE, PAIR, D), F32),
            vmem((RANK, D), F32),
            vmem((N, ROWS, 1, WIDE), F32),
            vmem((N, 2, ROWS, COLS), F32), vmem((N, 2, ROWS, COLS), F32),
            vmem((N, ROWS // 2, 2 * COLS), F32), vmem((N, ROWS // 2, 2 * COLS), F32),
            vmem((N, ROWS // 2, 2 * COLS), F32),
            vmem((2, LEFT, 128), F32), vmem((N, LEFT, 128), F32),
            vmem((COLS, D), F32),
            vmem((1, ROWS, WIDE), BF16), vmem((N, ROWS, WIDE), BF16),
            vmem((N, 4, ROWS), F32),
            dma((10,)), dma((10,)), dma((2,)), dma((10,)),
        ],
        compiler_params=pltpu.CompilerParams(
            collective_id=0, has_side_effects=True, vmem_limit_bytes=24 << 20
        ),
    )(
        *[
            pltpu.with_memory_space_constraint(array, pltpu.HBM)
            for array in (
                inner_embed, outer_embed, moment_embed, basis_t, inner_rows, outer_t,
                moment_t, inner_norms, outer_norms, moment_norms,
            )
        ]
    )

    new_e, new_me, new_a, new_ma, new_n, new_mn, replica = pl.pallas_call(
        write,
        out_shape=outs,
        in_specs=[on_chip] * 7,
        out_specs=[in_place] * 7,
        scratch_shapes=[dma((7,))],
        compiler_params=pltpu.CompilerParams(vmem_limit_bytes=4 << 20),
    )(*results)
    return new_e, new_me, new_a.T, new_ma.T, new_n, new_mn, replica


def solution(mesh):
    return jax.shard_map(
        on_device,
        mesh=mesh,
        in_specs=(
            P("group", "shard", None),
            P("shard", None),
            P("shard", None),
            P("shard", None),
            P("group", "shard", None),
            P(None, "shard"),
            P(None, "shard"),
            P("group", None, "shard"),
            P(None, "shard"),
            P(None, "shard"),
        ),
        out_specs=(
            P("shard", None),
            P("shard", None),
            P(None, "shard"),
            P(None, "shard"),
            P(None, "shard"),
            P(None, "shard"),
            P("shard", None),
        ),
        check_vma=False,
    )
```

```python
import math

import jax
import jax.numpy as jnp
from jax import lax
from jax.experimental import pallas as pl
from jax.experimental.pallas import tpu as pltpu
from jax.sharding import PartitionSpec as P

VOCAB = 15360
RANK = 64
D = 768
N = 8
PLANE = 32
RING = 16
ROWS = 12
COLS = 48
WIDE = N * COLS
TALL = N * ROWS
LEFT = 36
PAIR = RANK // PLANE
PARTS = 3
MESH = pl.DeviceIdType.MESH
HIGHEST = lax.Precision.HIGHEST
SCALE = 1.0 / math.sqrt(RANK * VOCAB)
F32 = jnp.float32
BF16 = jnp.bfloat16

C1, CZ, C3, P1, W, NR, SW, S2, AG, RP = range(10)
L_IE, L_OE, L_ME, L_BA, L_OA, L_MA, L_IA, L_IN, L_ON, L_MN = range(10)

G_STEPS = (4, 5, 3, 6, 2, 7, 1)
Z_STEPS = tuple(sorted(range(1, RING), key=lambda k: -min(k, RING - k)))
P_STEPS = tuple(
    sorted(
        [(i, j, k) for i in range(4) for j in range(4) for k in range(2)][1:],
        key=lambda t: -(min(t[0], 4 - t[0]) + min(t[1], 4 - t[1])),
    )
)


def nesterov(outer, moment, delta):
    moment_new = 0.5 * moment + delta
    return (outer - (delta + 0.5 * moment_new), moment_new)


def inside(g):
    return jnp.logical_and(g >= 2, g <= 5)


def turned(g, half, x):
    low = jnp.where(half == 0, g, 7 - g)
    turn = jnp.where(inside(g), g - 2, jnp.where(low < 2, low, low - 4))
    high = lax.rem(x // 2 + turn // 2, 2)
    return 2 * high + lax.rem(lax.rem(x, 2) + lax.rem(turn, 2), 2)


def across(g, b):
    half, x = b // 4, lax.rem(b, 4)
    to_half = jnp.where(inside(g), half, 1 - half)
    return jnp.where(inside(g), g, 7 - g), 4 * to_half + turned(g, half, x)


def second(g):
    return jnp.where(
        inside(g), lax.rem(g + 4, N), jnp.where(g < 4, g + 2, g - 2)
    )


def second_from(g, b):
    half, x = b // 4, lax.rem(b, 4)
    owner = jnp.where(
        inside(g), jnp.where(g < 4, g - 2, g + 2), lax.rem(g + 4, N)
    )
    from_half = jnp.where(inside(owner), half, 1 - half)
    return owner, 4 * from_half + turned(owner, from_half, x)


def exchange(
    inner_e, outer_e, mom_e, basis, inner_a, outer_a, mom_a, inner_n, outer_n, mom_n,
    o_e, o_me, o_a, o_ma, o_n, o_mn, rep,
    v_ie, v_oe, v_me, v_ba, v_oa, v_ma, v_on, v_mn,
    c_part, r_c1, c_own, r_cz, c_fin, r_c3, coef,
    r_p1, w_out, r_w, d_out, r_d, r_d2, d_all, r_ag, delta_t, rp_out, r_rp, r_norm,
    send, recv, once, local,
):
    g = lax.axis_index("group")
    s = lax.axis_index("shard")
    b, a = s // N, lax.rem(s, N)
    half, p = s // PLANE, lax.rem(s, PLANE)
    x, y, core = p // 8, lax.rem(p // 2, 4), lax.rem(p, 2)
    z = N * half + g
    far_g, far_b = across(g, b)
    from_g, from_b = second_from(g, b)

    def in_plane(step):
        i, j, k = step
        return 8 * lax.rem(x + i, 4) + 2 * lax.rem(y + j, 4) + lax.rem(core + k, 2)

    plane = [in_plane(step) for step in P_STEPS]
    ring = [lax.rem(z + k, RING) for k in Z_STEPS]
    line = [lax.rem(g + k, N) for k in G_STEPS]
    turns = [lax.rem(a + k, N) for k in range(N)]
    to_plane = [(g, PLANE * half + q) for q in plane]
    to_ring = [(lax.rem(q, N), PLANE * (q // N) + p) for q in ring]
    to_line = [(q, s) for q in line]
    to_swap = [(far_g, N * far_b + q) for q in turns]
    to_second = [(second(g), N * far_b + q) for q in turns]
    turn_first = jnp.where(lax.rem(g, 4) < 2, 3, 1)
    to_near = [
        (4 * (g // 4) + lax.rem(g + k, 4), s) for k in (turn_first, 2, 4 - turn_first)
    ]
    crossing = jnp.logical_or(far_b != b, far_g != g)

    barrier = pltpu.get_barrier_semaphore()

    def greet(device):
        pl.semaphore_signal(barrier, inc=1, device_id=device, device_id_type=MESH)

    for device in to_ring + to_swap[1:] + to_plane:
        greet(device)

    @pl.when(crossing)
    def _():
        greet(to_swap[0])

    def load(src, dst, sem):
        copy = pltpu.make_async_copy(src, dst, local.at[sem])
        copy.start()
        return copy

    def block(q):
        return inner_a.at[:, :, pl.ds(pl.multiple_of(q * WIDE, 128), WIDE)]

    ld_oa = load(outer_a, v_oa, L_OA)
    ld_ma = load(mom_a, v_ma, L_MA)
    ld_ie = load(inner_e.at[0], v_ie, L_IE)
    ld_oe = load(outer_e, v_oe, L_OE)
    ld_ba = load(basis, v_ba, L_BA)
    ld_ia = load(block(far_b), r_p1.at[g], L_IA)
    ld_in = load(inner_n.at[0], r_norm.at[g], L_IN)
    ld_on = load(outer_n, v_on, L_ON)
    ld_mn = load(mom_n, v_mn, L_MN)
    ld_me = load(mom_e, v_me, L_ME)

    def put(src, dst, phase, device, send_sem=None):
        pltpu.make_async_remote_copy(
            src_ref=src,
            dst_ref=dst,
            send_sem=send.at[phase] if send_sem is None else send_sem,
            recv_sem=recv.at[phase],
            device_id=device,
            device_id_type=MESH,
        ).start()

    def whole(ref, phase, count):
        part = ref.at[pl.ds(0, count)]
        return pltpu.make_async_remote_copy(
            src_ref=part,
            dst_ref=part,
            send_sem=send.at[phase],
            recv_sem=recv.at[phase],
            device_id=to_line[0],
            device_id_type=MESH,
        )

    def arrived(ref, phase):
        whole(ref, phase, ref.shape[0] - 1).wait_recv()

    def swap(src, dst, phase, turn):
        for k in range(1, N):
            put(src.at[turns[k]], dst.at[a], phase, to_swap[k])

        @pl.when(crossing)
        def _():
            put(src.at[a], dst.at[a], phase, to_swap[0], once.at[turn])

        @pl.when(jnp.logical_not(crossing))
        def _():
            dst[a] = src[a]

    def swap_arrived(ref, phase):
        @pl.when(crossing)
        def _():
            whole(ref, phase, N).wait_recv()

        @pl.when(jnp.logical_not(crossing))
        def _():
            whole(ref, phase, N - 1).wait_recv()

    pl.semaphore_wait(
        barrier, RING - 1 + PLANE - 1 + N - 1 + jnp.where(crossing, 1, 0)
    )

    for q, device in zip(line, to_line):
        put(block(across(q, b)[1]), r_p1.at[g], P1, device)

    ld_oa.wait()
    ld_ma.wait()
    for i, ref in enumerate((v_oa, v_ma)):
        state = ref[...]
        rows = state[:, :TALL]
        for j in range(1, N):
            rows = jnp.where(far_b == j, state[:, TALL * j : TALL * (j + 1)], rows)
        rows = rows.T
        for j in range(N):
            w_out[j, i] = rows[ROWS * j : ROWS * (j + 1), :]
    swap(w_out, r_w, W, 0)

    ld_ie.wait()
    ld_oe.wait()
    ld_ba.wait()
    part = jnp.dot(
        v_ba[...],
        v_oe[...] - v_ie[...],
        precision=HIGHEST,
        preferred_element_type=F32,
    )
    for j in range(PLANE):
        c_part[j] = part[PAIR * j : PAIR * (j + 1), :]
    for q, device in zip(plane, to_plane):
        put(c_part.at[q], r_c1.at[p], C1, device)
    r_c1[p] = c_part[p]
    for device in to_line:
        put(inner_n.at[0], r_norm.at[g], NR, device)

    swap_arrived(r_w, W)
    outer_wide = jnp.concatenate([r_w[j, 0] for j in range(N)], axis=1)
    mom_wide = jnp.concatenate([r_w[j, 1] for j in range(N)], axis=1)
    arrived(r_c1, C1)
    row = r_c1[0]
    for j in range(1, PLANE):
        row = row + r_c1[j]
    c_own[0] = row
    for device in to_ring:
        put(c_own.at[0], r_cz.at[z], CZ, device)
    r_cz[z] = row
    ld_ia.wait()
    arrived(r_p1, P1)
    total = outer_wide - r_p1[0, :, 0, :]
    for j in range(1, N):
        total = total + (outer_wide - r_p1[j, :, 0, :])
    delta = total * (1.0 / N)
    for j in range(N):
        chunk = delta[:, COLS * j : COLS * (j + 1)]
        d_out[j] = jnp.concatenate(
            [chunk[: ROWS // 2, :], chunk[ROWS // 2 :, :]], axis=1
        )
    for k in range(N):
        put(d_out.at[turns[k]], r_d2.at[a], S2, to_second[k])
    swap(d_out, r_d, SW, 1)
    replica = nesterov(outer_wide, mom_wide, delta)[0].astype(BF16)
    rp_out[0] = replica
    for device in to_line:
        put(rp_out.at[0], r_rp.at[far_b], RP, device)
    r_rp[far_b] = replica

    ld_in.wait()
    ld_on.wait()
    ld_mn.wait()
    arrived(r_norm, NR)
    outer_norm = v_on[...]
    total = outer_norm - r_norm[0]
    for j in range(1, N):
        total = total + (outer_norm - r_norm[j])
    o_n[...], o_mn[...] = nesterov(outer_norm, v_mn[...], total * (1.0 / N))

    def gather(ref, turn, rows):
        parts = []
        for j in range(N):
            parts += [ref[j, :, :COLS], ref[j, :, COLS:]]
        tall = jnp.concatenate(parts, axis=0).T
        rest = [tall[LEFT:, 32 * j : 32 * (j + 1)] for j in range(3)]
        tall = jnp.concatenate(
            [tall[:LEFT, :], jnp.concatenate(rest, axis=0)], axis=1
        )
        d_all[turn] = tall
        for device in to_near:
            put(d_all.at[turn], r_ag.at[rows], AG, device)
        r_ag[rows] = tall


    arrived(r_cz, CZ)
    row = r_cz[0]
    for j in range(1, RING):
        row = row + r_cz[j]
    row = row * (1.0 / N)
    c_fin[0] = row
    for device in to_plane:
        put(c_fin.at[0], r_c3.at[p], C3, device)
    r_c3[p] = row

    swap_arrived(r_d, SW)
    gather(r_d, 0, far_b)
    whole(r_d2, S2, N).wait_recv()
    gather(r_d2, 1, from_b)

    arrived(r_rp, RP)
    for j in range(N):
        rep[:, WIDE * j : WIDE * (j + 1)] = r_rp[j]

    ld_me.wait()
    arrived(r_c3, C3)
    for j in range(PLANE):
        coef[PAIR * j : PAIR * (j + 1), :] = r_c3[j]
    change = lax.dot_general(
        v_ba[...],
        coef[...],
        (((0,), (0,)), ((), ())),
        precision=HIGHEST,
        preferred_element_type=F32,
    ) * SCALE
    o_e[...], o_me[...] = nesterov(v_oe[...], v_me[...], change)

    whole(r_ag, AG, 6).wait_recv()
    for j in range(N):
        packed = r_ag[j]
        rest = [packed[12 * i : 12 * (i + 1), TALL:] for i in range(3)]
        delta_t[:LEFT, TALL * j : TALL * (j + 1)] = packed[:, :TALL]
        delta_t[LEFT:, TALL * j : TALL * (j + 1)] = jnp.concatenate(rest, axis=1)
    o_a[...], o_ma[...] = nesterov(v_oa[...], v_ma[...], delta_t[...])

    for ref, phase in (
        (r_c1, C1), (r_cz, CZ), (r_c3, C3), (r_p1, P1), (r_norm, NR), (r_rp, RP),
    ):
        whole(ref, phase, ref.shape[0] - 1).wait_send()
    for ref, phase, count in ((r_w, W, N - 1), (r_d, SW, N - 1), (r_d2, S2, N), (r_ag, AG, 6)):
        whole(ref, phase, count).wait_send()

    @pl.when(crossing)
    def _():
        for ref, turn in ((r_w, 0), (r_d, 1)):
            pltpu.make_async_remote_copy(
                src_ref=ref.at[0],
                dst_ref=ref.at[0],
                send_sem=once.at[turn],
                recv_sem=recv.at[W],
                device_id=to_line[0],
                device_id_type=MESH,
            ).wait_send()


def write(*refs):
    sems = refs[-1]
    pairs = []
    for src, dst in zip(refs[:7], refs[7:14]):
        rows = src.shape[0]
        step = rows // PARTS if rows % (8 * PARTS) == 0 else rows
        for first in range(0, rows, step):
            part = pl.ds(first, step)
            pairs.append((src.at[part, :], dst.at[part, :]))
    copies = [
        pltpu.make_async_copy(src, dst, sems.at[i])
        for i, (src, dst) in enumerate(pairs)
    ]
    for copy in copies:
        copy.start()
    for copy in copies:
        copy.wait()


def on_device(
    inner_embed, outer_embed, moment_embed, basis, inner_attn, outer_attn,
    moment_attn, inner_norms, outer_norms, moment_norms,
):
    vmem = pltpu.VMEM
    dma = pltpu.SemaphoreType.DMA
    basis_t, outer_t, moment_t = basis.T, outer_attn.T, moment_attn.T
    inner_rows = inner_attn.reshape(ROWS, 1, 4 * D)
    in_place = pl.BlockSpec(memory_space=pl.ANY)
    in_hbm = pl.BlockSpec(memory_space=pltpu.HBM)
    on_chip = pl.BlockSpec(memory_space=pltpu.VMEM)
    shape = jax.ShapeDtypeStruct
    vocab = outer_embed.shape[0]

    outs = [
        shape((vocab, D), F32), shape((vocab, D), F32), shape((COLS, D), F32),
        shape((COLS, D), F32), shape((4, ROWS), F32), shape((4, ROWS), F32),
        shape((ROWS, 4 * D), BF16),
    ]
    results = pl.pallas_call(
        exchange,
        out_shape=outs,
        in_specs=[in_hbm] * 10,
        out_specs=[on_chip] * 7,
        scratch_shapes=[
            vmem((vocab, D), F32), vmem((vocab, D), F32), vmem((vocab, D), F32),
            vmem((RANK, vocab), F32), vmem((COLS, D), F32), vmem((COLS, D), F32),
            vmem((4, ROWS), F32), vmem((4, ROWS), F32),
            vmem((PLANE, PAIR, D), F32), vmem((PLANE, PAIR, D), F32),
            vmem((1, PAIR, D), F32), vmem((RING, PAIR, D), F32),
            vmem((1, PAIR, D), F32), vmem((PLANE, PAIR, D), F32),
            vmem((RANK, D), F32),
            vmem((N, ROWS, 1, WIDE), F32),
            vmem((N, 2, ROWS, COLS), F32), vmem((N, 2, ROWS, COLS), F32),
            vmem((N, ROWS // 2, 2 * COLS), F32), vmem((N, ROWS // 2, 2 * COLS), F32),
            vmem((N, ROWS // 2, 2 * COLS), F32),
            vmem((2, LEFT, 128), F32), vmem((N, LEFT, 128), F32),
            vmem((COLS, D), F32),
            vmem((1, ROWS, WIDE), BF16), vmem((N, ROWS, WIDE), BF16),
            vmem((N, 4, ROWS), F32),
            dma((10,)), dma((10,)), dma((2,)), dma((10,)),
        ],
        compiler_params=pltpu.CompilerParams(
            collective_id=0, has_side_effects=True, vmem_limit_bytes=24 << 20
        ),
    )(
        *[
            pltpu.with_memory_space_constraint(array, pltpu.HBM)
            for array in (
                inner_embed, outer_embed, moment_embed, basis_t, inner_rows, outer_t,
                moment_t, inner_norms, outer_norms, moment_norms,
            )
        ]
    )

    new_e, new_me, new_a, new_ma, new_n, new_mn, replica = pl.pallas_call(
        write,
        out_shape=outs,
        in_specs=[on_chip] * 7,
        out_specs=[in_place] * 7,
        scratch_shapes=[dma((7 * PARTS,))],
        compiler_params=pltpu.CompilerParams(vmem_limit_bytes=4 << 20),
    )(*results)
    return new_e, new_me, new_a.T, new_ma.T, new_n, new_mn, replica


def solution(mesh):
    return jax.shard_map(
        on_device,
        mesh=mesh,
        in_specs=(
            P("group", "shard", None),
            P("shard", None),
            P("shard", None),
            P("shard", None),
            P("group", "shard", None),
            P(None, "shard"),
            P(None, "shard"),
            P("group", None, "shard"),
            P(None, "shard"),
            P(None, "shard"),
        ),
        out_specs=(
            P("shard", None),
            P("shard", None),
            P(None, "shard"),
            P(None, "shard"),
            P(None, "shard"),
            P(None, "shard"),
            P("shard", None),
        ),
        check_vma=False,
    )
```
